256 devices in a mesh: cache: 8 (over z_hi, core), expert: 32 (over x, z_lo, y).
Axes of the slice: x: 4, y: 4, z: 8 (z_hi: 4, z_lo: 2; z = z_hi * 2 + z_lo), core: 2. Of those that a mesh axis runs over, the one named last changes fastest.
Arguments:
- queries: bfloat16 [2, 128, 2048], P(None, 'expert'), may hold values from -16 to 16
- k_cache: bfloat16 [128, 8192, 256], P('expert', 'cache'), may hold values from -6 to 6
- v_cache: bfloat16 [128, 8192, 256], P('expert', 'cache'), may hold values from -6 to 6
- lengths: int32 [128], P('expert'), may hold values from 1 to 8190
- w_out: bfloat16 [2048, 2880], P('cache'), may hold values from -0.125 to 0.125
- norm_gain: float32 [2880], replicated, may hold values from 0.25 to 1.75
- w_gate: bfloat16 [32, 2880, 1440], P('cache', 'expert'), may hold values from -0.109375 to 0.109375
- w_up: bfloat16 [32, 2880, 1440], P('cache', 'expert'), may hold values from -0.109375 to 0.109375
- w_down: bfloat16 [32, 1440, 2880], P('cache', None, 'expert'), may hold values from -0.15625 to 0.15625
- expert_ids: int32 [2, 128, 4], P(None, 'expert'), may hold values from 0 to 31, all different within a row; in each aligned block of 4 rows (0 to 3, 4 to 7, ..., all dimensions but the last counted through in order) at most 2 rows name the same one
- gate_weights: float32 [2, 128, 4], P(None, 'expert'), may hold values from 0.1 to 1
Outputs:
- mixed: bfloat16 [2, 128, 2880], P(None, 'expert')
- gate_owner: bfloat16 [32, 2880, 1440], P('expert', None, 'cache')
- up_owner: bfloat16 [32, 2880, 1440], P('expert', None, 'cache')
- down_owner: bfloat16 [32, 1440, 2880], P('expert', 'cache')
The draws below stay inside these ranges and needn't reach their ends.
Inputs may be any that keep to these rules, and one draw needn't show every extreme that they name: `expert_ids`: in each step the 4 rows of one index of expert name one expert at most 2 times; a row names 4 different experts.
All inputs are finite; a program needn't handle non-finite values.
Results may differ from the reference program's by a relative error of at most 0.015.
Values may be sent and summed in bfloat16 or wider, within the bound.
No kernel may reach another device: no remote copies, remote signals or barrier semaphores. Data moves between devices by JAX's collectives and lax.ppermute only.
A program may use at most 64 MiB of HBM per device.

```python
import math
import jax
import jax.numpy as jnp
import numpy as np
from jax import lax

D = 2880
FF = 1440
QH = 32
KVH = 4
HD = 64
TOP = 4
STEPS = 2
ROWS_DEV = 4
EXPERTS = 32
CAP = 2
ROWS = 128
LENGTH = 8192


def draw_queries(key, part):
    result = 2.5 * jax.random.truncated_normal(jax.random.fold_in(key, 1), -6.0, 6.0, (STEPS, ROWS, QH * HD), jnp.float32)
    return result.astype(jnp.bfloat16)


def draw_k_cache(key, part):
    result = jax.random.truncated_normal(jax.random.fold_in(key, 2), -6.0, 6.0, (ROWS, LENGTH, KVH * HD), jnp.float32)
    return result.astype(jnp.bfloat16)


def place_ends(values, rng, low, top_value):
    longest = values.shape.index(max(values.shape))
    spots = []
    for shift in (0, 1):
        where = [jax.random.randint(jax.random.fold_in(rng, axis), (), 0, length) for axis, length in enumerate(values.shape)]
        where[longest] = (where[longest] + shift) % values.shape[longest]
        spots.append(tuple(where))
    return values.at[spots[0]].set(low).at[spots[1]].set(top_value)


def steps_of(own_key, dims, cuts, smallest, top_value):
    gain, own = 1.0, jax.random.fold_in(own_key, 6)
    for dim, shards_of in cuts:
        draws = jnp.exp(jax.random.uniform(jax.random.fold_in(own, dim), (shards_of,), jnp.float32, smallest / len(cuts), top_value / len(cuts)))
        gain = gain * jnp.repeat(draws, dims[dim] // shards_of).reshape([-1 if axis == dim else 1 for axis in range(len(dims))])
    return gain


def deal_out(own_key, own, number, rows, count, top, bound, skew):
    sequence = jax.random.permutation(own_key, count)
    heavy_load, common = shares(count, rows * top, bound, skew, True), shares(count, rows * top, bound, skew, False)
    places = jnp.arange(count)

    def named(tallies, rotation):
        used = int((tallies > 0).sum())
        fixed = max(1, used // 4)
        moved = fixed + (places - fixed + rotation * (used - fixed)) % max(1, count - fixed)
        return jnp.zeros((count,), jnp.int32).at[sequence[jnp.where(places < fixed, places, moved)]].set(jnp.asarray(tallies, jnp.int32))

    tallies = jnp.where(number % 4 == 0, named(heavy_load, number // 4), named(common, number - number // 4 - 1))
    mixed = jax.random.permutation(jax.random.fold_in(own, 3), count)
    donor, taker = mixed[0:count // 2 * 2:2], mixed[1:count // 2 * 2:2]
    margin = jnp.minimum(tallies[donor] - 1, bound - tallies[taker]) // 2
    margin = jnp.where((donor == sequence[0]) | (taker == sequence[0]) | (tallies[taker] == 0), 0, jnp.maximum(margin, 0))
    moved = jax.random.randint(jax.random.fold_in(own, 4), (count // 2,), 0, 1 << 20) % (margin + 1)
    tallies = tallies.at[donor].add(-moved).at[taker].add(moved)
    labels = jnp.searchsorted(jnp.cumsum(tallies), jnp.arange(rows * top), side="right").astype(jnp.int32)
    listing = labels.reshape(top, rows).T
    listing = listing[jax.random.permutation(jax.random.fold_in(own, 1), rows)]
    rotation = jax.random.randint(jax.random.fold_in(own, 2), (rows, 1), 0, top)
    return jnp.take_along_axis(listing, (jnp.arange(top)[None, :] + rotation) % top, axis=1)


def shares(count, total, most, skew, full):
    weights = [(1 << 20) // math.isqrt(grade ** skew) + 1 for grade in range(1, count + 1)]
    largest = most if full else min(most, max(-(-total // count), total * weights[0] // sum(weights)))
    least = 1 if total - largest >= count - 1 else 0
    holding, spare = [largest] + [least] * (count - 1), total - largest - least * (count - 1)
    while spare > 0:
        free = [i for i in range(1, count) if holding[i] < largest] or [i for i in range(1, count) if holding[i] < most]
        whole, left = sum([weights[i] for i in free]), spare
        for i in free:
            addition = min(most - holding[i], max(1, left * weights[i] // whole), spare)
            holding[i] = holding[i] + addition
            spare = spare - addition
    return np.array(holding)


def gaussian(key, dims, deviation, reach, shards=(), kind=jnp.bfloat16):
    values = deviation * jax.random.normal(key, dims, jnp.float32)
    if shards:
        values = values * steps_of(key, dims, shards, -0.22, 0.18)
    return jnp.clip(values, -reach, reach).astype(kind)


def setup_inputs(seed: int = 0) -> dict:
    splits = jax.random.split(jax.random.key(seed), 12)
    queries = draw_queries(jax.random.fold_in(splits[11], 71), 0)
    k_cache = draw_k_cache(jax.random.fold_in(splits[11], 71), 0)
    v_cache = gaussian(splits[2], (ROWS, LENGTH, KVH * HD), 1.0, 6.0, ((0, 32), (1, 8)))
    lengths = place_ends(jax.random.randint(splits[3], (ROWS,), 1, LENGTH - 1), jax.random.fold_in(splits[3], 1), 1, (LENGTH - 1) - 1).astype(jnp.int32)
    w_out = gaussian(splits[4], (QH * HD, D), (QH * HD) ** -0.5, 0.125, ((0, 8),))
    norm_gain = jnp.clip(1.0 + 0.15 * jax.random.normal(splits[5], (D,), jnp.float32), 0.25, 1.75)
    w_gate = gaussian(splits[6], (EXPERTS, D, FF), D ** -0.5, 0.109375, ((0, 8), (1, 32)))
    w_up = gaussian(splits[7], (EXPERTS, D, FF), D ** -0.5, 0.109375, ((0, 8), (1, 32)))
    w_down = gaussian(splits[8], (EXPERTS, FF, D), FF ** -0.5, 0.15625, ((0, 8), (2, 32)))
    expert_ids_keys = jax.random.split(jax.random.fold_in(splits[9], 1), STEPS * ROWS // ROWS_DEV)
    expert_ids_turns = jax.random.permutation(jax.random.fold_in(splits[9], 3), STEPS * ROWS // ROWS_DEV)
    expert_ids = jax.vmap(lambda own, number: deal_out(jax.random.fold_in(splits[9], 2), own, number, ROWS_DEV, EXPERTS, TOP, CAP, 2))(expert_ids_keys, expert_ids_turns).reshape((STEPS, ROWS, TOP))
    gate_weights = jnp.clip(0.1 + 0.9 * jax.random.uniform(splits[10], (STEPS, ROWS, TOP), jnp.float32) ** steps_of(splits[10], (STEPS, ROWS, TOP), ((1, 32),), -0.2, 0.2), 0.1, 1.0)
    return {"queries": queries, "k_cache": k_cache, "v_cache": v_cache, "lengths": lengths, "w_out": w_out, "norm_gain": norm_gain, "w_gate": w_gate, "w_up": w_up, "w_down": w_down, "expert_ids": expert_ids, "gate_weights": gate_weights}


def attend_row(query_row, key_row, value_row, length_row):
    group_size = QH // KVH
    query_heads = query_row.astype(jnp.float32).reshape(STEPS, KVH, group_size, HD)
    key_heads = key_row.astype(jnp.float32).reshape(LENGTH, KVH, HD)
    value_heads = value_row.astype(jnp.float32).reshape(LENGTH, KVH, HD)
    scores = jnp.einsum('shgd,phd->shgp', query_heads, key_heads) / math.sqrt(HD)
    limit = length_row + jnp.arange(STEPS, dtype=jnp.int32) + 1
    visible = jnp.arange(LENGTH, dtype=jnp.int32)[None, :] < limit[:, None]
    visible = visible[:, None, None, :]
    highest = lax.optimization_barrier(jnp.max(jnp.where(visible, scores, -1e+30), axis=-1, keepdims=True))
    weights = jnp.where(visible, jnp.exp(scores - highest), 0.0)
    mass = lax.optimization_barrier(jnp.sum(weights, axis=-1))
    rounded = lax.optimization_barrier(weights.astype(jnp.bfloat16)).astype(jnp.float32)
    accum = jnp.einsum('shgp,phd->shgd', rounded, value_heads)
    return (accum / mass[..., None]).reshape(STEPS, QH * HD).astype(jnp.bfloat16)

def reference(queries, k_cache, v_cache, lengths, w_out, norm_gain, w_gate, w_up, w_down, expert_ids, gate_weights):
    outputs = lax.map(lambda inputs: attend_row(*inputs), (jnp.swapaxes(queries, 0, 1), k_cache, v_cache, lengths))
    heads_out = jnp.swapaxes(outputs, 0, 1).reshape(STEPS * ROWS, QH * HD)
    attention = jnp.dot(heads_out, w_out, preferred_element_type=jnp.float32)
    scale = lax.rsqrt(lax.optimization_barrier(jnp.mean(attention * attention, axis=-1, keepdims=True)) + 1e-05)
    normed = (attention * scale * norm_gain).astype(jnp.bfloat16)
    picked = (expert_ids[..., None] == jnp.arange(EXPERTS, dtype=jnp.int32)).astype(jnp.float32)
    coefficient = lax.optimization_barrier(jnp.sum(picked * gate_weights[..., None], axis=2)).reshape(STEPS * ROWS, EXPERTS)

    def one_expert(running, inputs):
        gate_matrix, up_matrix, down_matrix, column = inputs
        gate_value = jnp.dot(normed, gate_matrix, preferred_element_type=jnp.float32)
        up_value = jnp.dot(normed, up_matrix, preferred_element_type=jnp.float32)
        hidden = (jax.nn.silu(gate_value) * up_value).astype(jnp.bfloat16)
        expert_out = jnp.dot(hidden, down_matrix, preferred_element_type=jnp.float32).astype(jnp.bfloat16)
        expert_out = lax.optimization_barrier(expert_out).astype(jnp.float32)
        return (running + column[:, None] * expert_out, None)
    start = jnp.zeros((STEPS * ROWS, D), jnp.float32)
    combined, _ = lax.scan(one_expert, start, (w_gate, w_up, w_down, coefficient.T))
    mixed = (attention + combined).astype(jnp.bfloat16).reshape(STEPS, ROWS, D)
    return (mixed, w_gate, w_up, w_down)
```

```python
import math

import jax
import jax.numpy as jnp
from jax import lax
from jax.experimental import pallas as pl
from jax.experimental.pallas import tpu as pltpu
from jax.sharding import PartitionSpec as P

D = 2880
QH = 32
KVH = 4
HD = 64
TOP = 4
NEG = -1e30
BF = jnp.bfloat16
F32 = jnp.float32
NT = (((1,), (1,)), ((), ()))
PARAMS = pltpu.CompilerParams(vmem_limit_bytes=48 << 20)


def pack_kernel(gate_ref, up_ref, down_ref, out_ref):
    blocks, experts = out_ref.shape[0], out_ref.shape[1]
    depth = gate_ref.shape[0]
    half = depth // 2
    width = gate_ref.shape[2] // blocks
    for k in range(experts):
        gate = gate_ref[:, k, :]
        up = up_ref[:, k, :]
        down = down_ref[:, k, :]
        for c in range(blocks):
            cut = slice(c * width, (c + 1) * width)
            out_ref[c, k, 0:depth, :] = jnp.concatenate([gate[:, cut], up[:, cut]], axis=1)
            out_ref[c, k, depth : depth + half, :] = jnp.concatenate(
                [down[0:half, cut], down[half:depth, cut]], axis=1
            )


def pack(gate, up, down, blocks):
    depth, experts, width = gate.shape
    rows = -(-(depth + depth // 2) // 8) * 8
    return pl.pallas_call(
        pack_kernel,
        out_shape=jax.ShapeDtypeStruct((blocks, experts, rows, 2 * width // blocks), BF),
        compiler_params=PARAMS,
        name="pack",
    )(gate, up, down)


def attend_kernel(length_ref, base_ref, query_ref, key_ref, value_ref, out_ref):
    row = pl.program_id(0)
    heads = query_ref.shape[1]
    positions = key_ref.shape[1]
    scores = lax.dot_general(query_ref[0], key_ref[0], NT, preferred_element_type=F32)
    scores = scores * (1.0 / math.sqrt(HD))
    position = base_ref[0] + lax.broadcasted_iota(jnp.int32, (heads, positions), 1)
    step = (lax.broadcasted_iota(jnp.int32, (heads, positions), 0) >= heads // 2).astype(jnp.int32)
    visible = position < length_ref[row] + 1 + step
    highest = jnp.max(jnp.where(visible, scores, NEG), axis=-1, keepdims=True)
    highest = highest.astype(BF).astype(F32)
    weights = jnp.where(visible, jnp.exp(scores - highest), 0.0)
    mass = jnp.sum(weights, axis=-1, keepdims=True)
    wide = jnp.dot(weights.astype(BF), value_ref[0], preferred_element_type=F32)
    group = heads // (2 * KVH)
    own = (lax.broadcasted_iota(jnp.int32, (heads, HD), 0) // group) % KVH
    accum = jnp.zeros((heads, HD), F32)
    for h in range(KVH):
        accum = accum + jnp.where(own == h, wide[:, h * HD : (h + 1) * HD], 0.0)
    mass_high = mass.astype(BF).astype(F32)
    lane = lax.broadcasted_iota(jnp.int32, (heads, HD), 1)
    extra = jnp.where(lane == 0, highest, jnp.where(lane == 1, mass_high, jnp.where(lane == 2, mass - mass_high, 0.0)))
    out_ref[0] = jnp.concatenate([accum, extra], axis=1).astype(BF)


def attend(lengths, base, query, keys, values):
    rows, heads, width = query.shape
    positions = keys.shape[1]
    grid_spec = pltpu.PrefetchScalarGridSpec(
        num_scalar_prefetch=2,
        grid=(rows,),
        in_specs=[
            pl.BlockSpec((1, heads, width), lambda r, *_: (r, 0, 0)),
            pl.BlockSpec((1, positions, width), lambda r, *_: (r, 0, 0)),
            pl.BlockSpec((1, positions, width), lambda r, *_: (r, 0, 0)),
        ],
        out_specs=pl.BlockSpec((1, heads, 2 * HD), lambda r, *_: (r, 0, 0)),
    )
    return pl.pallas_call(
        attend_kernel,
        grid_spec=grid_spec,
        out_shape=jax.ShapeDtypeStruct((rows, heads, 2 * HD), BF),
        compiler_params=PARAMS,
        name="attend",
    )(lengths, base, query, keys, values)


def expert_kernel(slots_ref, weights_ref, out_ref, first_ref, second_ref):
    sources = weights_ref.shape[0]
    depth = first_ref.shape[0] // sources
    half = depth // 2
    rows = depth + half
    width = second_ref.shape[1]
    for j in range(sources):
        block = weights_ref[j]
        first_ref[j * depth : (j + 1) * depth, :] = block[0:depth]
        second_ref[j * depth : j * depth + half, :] = block[depth:rows, 0:width]
        second_ref[j * depth + half : (j + 1) * depth, :] = block[depth:rows, width : 2 * width]
    slots = slots_ref[...].reshape(out_ref.shape[0] * out_ref.shape[1], out_ref.shape[2])
    both = jnp.dot(slots, first_ref[...], preferred_element_type=F32)
    gate = both[:, 0:width]
    up = both[:, width : 2 * width]
    hidden = (gate * jax.nn.sigmoid(gate) * up).astype(BF)
    out = lax.dot_general(hidden, second_ref[...], NT, preferred_element_type=F32)
    out_ref[...] = out.astype(BF).reshape(out_ref.shape)


def expert(slots, weights):
    sources, width = weights.shape[0], weights.shape[2]
    depth = slots.shape[-1] // sources
    return pl.pallas_call(
        expert_kernel,
        out_shape=jax.ShapeDtypeStruct(slots.shape, BF),
        scratch_shapes=[
            pltpu.VMEM((sources * depth, width), BF),
            pltpu.VMEM((sources * depth, width // 2), BF),
        ],
        compiler_params=PARAMS,
        name="expert",
    )(slots, weights)


def owner_kernel(weights_ref, gate_ref, up_ref, down_ref, first_ref, second_ref):
    sources = weights_ref.shape[0]
    depth = first_ref.shape[0] // sources
    half = depth // 2
    rows = depth + half
    width = second_ref.shape[1]
    for j in range(sources):
        block = weights_ref[j]
        first_ref[j * depth : (j + 1) * depth, :] = block[0:depth]
        second_ref[j * depth : j * depth + half, :] = block[depth:rows, 0:width]
        second_ref[j * depth + half : (j + 1) * depth, :] = block[depth:rows, width : 2 * width]
    row = lax.broadcasted_iota(jnp.int32, (width, 2 * width), 0)
    lane = lax.broadcasted_iota(jnp.int32, (width, 2 * width), 1)
    first = first_ref[...]
    pick = (row == lane).astype(BF)
    gate_ref[...] = lax.dot_general(pick, first, NT, preferred_element_type=F32).astype(BF)
    pick = (row + width == lane).astype(BF)
    up_ref[...] = lax.dot_general(pick, first, NT, preferred_element_type=F32).astype(BF)
    row = lax.broadcasted_iota(jnp.int32, (width, width), 0)
    lane = lax.broadcasted_iota(jnp.int32, (width, width), 1)
    pick = (row == lane).astype(BF)
    down_ref[...] = lax.dot_general(pick, second_ref[...], NT, preferred_element_type=F32).astype(BF)


def owner(weights):
    sources, width = weights.shape[0], weights.shape[2]
    depth = D // sources
    shape = jax.ShapeDtypeStruct((width // 2, sources * depth), BF)
    return pl.pallas_call(
        owner_kernel,
        out_shape=(shape, shape, shape),
        scratch_shapes=[
            pltpu.VMEM((sources * depth, width), BF),
            pltpu.VMEM((sources * depth, width // 2), BF),
        ],
        compiler_params=PARAMS,
        name="owner",
    )(weights)


def shards(
    queries,
    k_cache,
    v_cache,
    lengths,
    w_out,
    norm_gain,
    w_gate,
    w_up,
    w_down,
    expert_ids,
    gate_weights,
):
    cache_count = lax.axis_size("cache")
    cache_place = lax.axis_index("cache")
    step_count = queries.shape[0]
    row_count, positions = k_cache.shape[0], k_cache.shape[1]
    group_size = QH // KVH

    packed = pack(
        jnp.transpose(w_gate, (1, 0, 2)),
        jnp.transpose(w_up, (1, 0, 2)),
        jnp.transpose(w_down, (2, 0, 1)),
        cache_count,
    )
    packed, queries = lax.optimization_barrier((packed, queries))
    moved = lax.all_to_all(packed, "cache", split_axis=0, concat_axis=0, tiled=True)

    query = queries.reshape(step_count, row_count, KVH, group_size, HD)
    query = jnp.transpose(query, (1, 0, 2, 3, 4))
    eye = jnp.eye(KVH, dtype=BF)
    query = query[:, :, :, :, None, :] * eye[None, None, :, None, :, None]
    query = query.reshape(row_count, step_count * QH, KVH * HD)
    base = (cache_place * positions).astype(jnp.int32).reshape(1)
    part = attend(lengths, base, query, k_cache, v_cache)
    parts = lax.all_gather(part, "cache", axis=0)
    own_heads = QH // cache_count
    parts = parts.reshape(cache_count, row_count, step_count, QH, 2 * HD)
    parts = lax.dynamic_slice_in_dim(parts, cache_place * own_heads, own_heads, 3).astype(F32)
    part_high = parts[..., HD : HD + 1]
    part_mass = parts[..., HD + 1 : HD + 2] + parts[..., HD + 2 : HD + 3]
    factor = jnp.exp(part_high - jnp.max(part_high, axis=0))
    own_out = jnp.sum(parts[..., 0:HD] * factor, axis=0) / jnp.sum(part_mass * factor, axis=0)
    own_rows = jnp.transpose(own_out.astype(BF), (1, 0, 2, 3)).reshape(step_count * row_count, own_heads * HD)
    projected = jnp.dot(own_rows, w_out, preferred_element_type=F32).astype(BF)
    attention = jnp.sum(lax.all_gather(projected, "cache", axis=0).astype(F32), axis=0)
    scale = lax.rsqrt(jnp.mean(attention * attention, axis=-1, keepdims=True) + 1e-05)
    normed = (attention * scale * norm_gain).astype(BF).reshape(step_count, row_count, D)

    experts_total = w_gate.shape[0] * cache_count
    capacity = max(2, (row_count * TOP + experts_total - 1) // experts_total)
    expert_range = jnp.arange(experts_total, dtype=jnp.int32)
    onehot = (expert_ids[..., None] == expert_range).astype(F32)
    chosen = jnp.sum(onehot, axis=2)
    gate_map = jnp.sum(onehot * gate_weights[..., None], axis=2)
    earlier = jnp.tril(jnp.ones((row_count, row_count), F32), -1)
    ranks = jnp.einsum("rq,sqe->sre", earlier, chosen, precision=lax.Precision.HIGHEST)
    slot_table = (ranks[..., None] == jnp.arange(capacity, dtype=F32)).astype(F32) * chosen[..., None]
    outgoing = jnp.einsum("srec,srd->escd", slot_table.astype(BF), normed, preferred_element_type=F32)
    outgoing = outgoing.astype(BF).reshape(experts_total, step_count * capacity, D)
    slots = lax.all_to_all(outgoing, "expert", split_axis=0, concat_axis=0, tiled=True)

    moved = moved.reshape(experts_total, moved.shape[2], moved.shape[3])
    arrived = lax.all_to_all(moved, "expert", split_axis=0, concat_axis=0, tiled=True)
    partial_out = expert(slots, arrived)
    returned = lax.all_to_all(partial_out, "expert", split_axis=0, concat_axis=0, tiled=True)
    arrived, partial_out = lax.optimization_barrier((arrived, partial_out))
    gate_owner, up_owner, down_owner = owner(arrived)

    returned = returned.reshape(experts_total, step_count, capacity, D)
    combined = jnp.einsum(
        "srec,escd->srd",
        slot_table * gate_map[..., None],
        returned.astype(F32),
        precision=lax.Precision.HIGHEST,
    )
    shares = lax.all_gather(combined.astype(BF), "cache", axis=0)
    total = jnp.sum(shares.astype(F32), axis=0) + attention.reshape(step_count, row_count, D)
    mixed = total.astype(BF)
    return (mixed, gate_owner.T[None], up_owner.T[None], down_owner[None])


def solution(mesh):
    return jax.shard_map(
        shards,
        mesh=mesh,
        in_specs=(
            P(None, "expert", None),
            P("expert", "cache", None),
            P("expert", "cache", None),
            P("expert"),
            P("cache", None),
            P(),
            P("cache", "expert", None),
            P("cache", "expert", None),
            P("cache", None, "expert"),
            P(None, "expert", None),
            P(None, "expert", None),
        ),
        out_specs=(
            P(None, "expert", None),
            P("expert", None, "cache"),
            P("expert", None, "cache"),
            P("expert", "cache", None),
        ),
        check_vma=False,
    )
```

```python
import math

import jax
import jax.numpy as jnp
import numpy as np
from jax import lax
from jax.experimental import pallas as pl
from jax.experimental.pallas import tpu as pltpu
from jax.sharding import Mesh
from jax.sharding import PartitionSpec as P

D = 2880
QH = 32
KVH = 4
HD = 64
TOP = 4
NEG = -1e30
BF = jnp.bfloat16
F32 = jnp.float32
NT = (((1,), (1,)), ((), ()))
CACHE = ("zh", "core")
EXPERT = ("x", "zl", "y")
HI_STEPS = (2, 1, 3, 0)
PARAMS = pltpu.CompilerParams(vmem_limit_bytes=48 << 20)


def pack_kernel(place_ref, gate_ref, up_ref, down_ref, *refs):
    out_refs, block_ref, sems = refs[:-2], refs[-2], refs[-1]
    blocks, experts = block_ref.shape[0], block_ref.shape[1]
    depth = gate_ref.shape[0]
    half = depth // 2
    width = gate_ref.shape[2] // blocks
    for k in range(experts):
        gate = gate_ref[:, k, :]
        up = up_ref[:, k, :]
        down = down_ref[:, k, :]
        for c in range(blocks):
            cut = slice(c * width, (c + 1) * width)
            block_ref[c, k, 0:depth, :] = jnp.concatenate([gate[:, cut], up[:, cut]], axis=1)
            block_ref[c, k, depth : depth + half, :] = jnp.concatenate(
                [down[0:half, cut], down[half:depth, cut]], axis=1
            )
    copies = [
        pltpu.make_async_copy(block_ref.at[place_ref[i]], out_refs[i], sems.at[i]) for i in range(blocks)
    ]
    for copy in copies:
        copy.start()
    for copy in copies:
        copy.wait()


def pack(places, gate, up, down):
    depth, experts, width = gate.shape
    blocks = places.shape[0]
    rows = -(-(depth + depth // 2) // 8) * 8
    shape = (experts, rows, 2 * width // blocks)
    whole = pl.BlockSpec(gate.shape, lambda i, *_: (0, 0, 0))
    grid_spec = pltpu.PrefetchScalarGridSpec(
        num_scalar_prefetch=1,
        grid=(1,),
        in_specs=[whole, whole, whole],
        out_specs=[pl.BlockSpec(memory_space=pltpu.HBM)] * blocks,
        scratch_shapes=[pltpu.VMEM((blocks, *shape), BF), pltpu.SemaphoreType.DMA((blocks,))],
    )
    return pl.pallas_call(
        pack_kernel,
        grid_spec=grid_spec,
        out_shape=[jax.ShapeDtypeStruct(shape, BF)] * blocks,
        compiler_params=PARAMS,
        name="pack",
    )(places, gate, up, down)


def join_kernel(place_ref, *refs):
    in_refs, out_ref, sems = refs[:-2], refs[-2], refs[-1]
    experts = in_refs[0].shape[0]
    copies = [
        pltpu.make_async_copy(in_ref, out_ref.at[pl.ds(place_ref[i] * experts, experts)], sems.at[i])
        for i, in_ref in enumerate(in_refs)
    ]
    for copy in copies:
        copy.start()
    for copy in copies:
        copy.wait()


def join(places, blocks):
    experts, rows, width = blocks[0].shape
    count = len(blocks)
    anywhere = pl.BlockSpec(memory_space=pltpu.HBM)
    grid_spec = pltpu.PrefetchScalarGridSpec(
        num_scalar_prefetch=1,
        grid=(1,),
        in_specs=[anywhere] * count,
        out_specs=anywhere,
        scratch_shapes=[pltpu.SemaphoreType.DMA((count,))],
    )
    return pl.pallas_call(
        join_kernel,
        grid_spec=grid_spec,
        out_shape=jax.ShapeDtypeStruct((count * experts, rows, width), BF),
        compiler_params=PARAMS,
        name="join",
    )(places, *blocks)


def attend_kernel(length_ref, base_ref, query_ref, key_ref, value_ref, out_ref):
    row = pl.program_id(0)
    heads = query_ref.shape[1]
    positions = key_ref.shape[1]
    scores = lax.dot_general(query_ref[0], key_ref[0], NT, preferred_element_type=F32)
    scores = scores * (1.0 / math.sqrt(HD))
    position = base_ref[0] + lax.broadcasted_iota(jnp.int32, (heads, positions), 1)
    step = (lax.broadcasted_iota(jnp.int32, (heads, positions), 0) >= heads // 2).astype(jnp.int32)
    visible = position < length_ref[row] + 1 + step
    highest = jnp.max(jnp.where(visible, scores, NEG), axis=-1, keepdims=True)
    highest = highest.astype(BF).astype(F32)
    weights = jnp.where(visible, jnp.exp(scores - highest), 0.0)
    mass = jnp.sum(weights, axis=-1, keepdims=True)
    wide = jnp.dot(weights.astype(BF), value_ref[0], preferred_element_type=F32)
    group = heads // (2 * KVH)
    own = (lax.broadcasted_iota(jnp.int32, (heads, HD), 0) // group) % KVH
    accum = jnp.zeros((heads, HD), F32)
    for h in range(KVH):
        accum = accum + jnp.where(own == h, wide[:, h * HD : (h + 1) * HD], 0.0)
    mass_high = mass.astype(BF).astype(F32)
    lane = lax.broadcasted_iota(jnp.int32, (heads, HD), 1)
    extra = jnp.where(lane == 0, highest, jnp.where(lane == 1, mass_high, jnp.where(lane == 2, mass - mass_high, 0.0)))
    out_ref[0] = jnp.concatenate([accum, extra], axis=1).astype(BF)


def attend(lengths, base, query, keys, values):
    rows, heads, width = query.shape
    positions = keys.shape[1]
    grid_spec = pltpu.PrefetchScalarGridSpec(
        num_scalar_prefetch=2,
        grid=(rows,),
        in_specs=[
            pl.BlockSpec((1, heads, width), lambda r, *_: (r, 0, 0)),
            pl.BlockSpec((1, positions, width), lambda r, *_: (r, 0, 0)),
            pl.BlockSpec((1, positions, width), lambda r, *_: (r, 0, 0)),
        ],
        out_specs=pl.BlockSpec((1, heads, 2 * HD), lambda r, *_: (r, 0, 0)),
    )
    return pl.pallas_call(
        attend_kernel,
        grid_spec=grid_spec,
        out_shape=jax.ShapeDtypeStruct((rows, heads, 2 * HD), BF),
        compiler_params=PARAMS,
        name="attend",
    )(lengths, base, query, keys, values)


def stack(low_ref, high_ref, first_ref, second_ref):
    per = 4
    width = second_ref.shape[1]
    depth = first_ref.shape[0] // (2 * low_ref.shape[0])
    half = depth // 2
    rows = depth + half
    for i in range(low_ref.shape[0]):
        for z, ref in enumerate((low_ref, high_ref)):
            block = ref[i]
            at = ((i // per * 2 + z) * per + i % per) * depth
            first_ref[at : at + depth, :] = block[0:depth]
            second_ref[at : at + half, :] = block[depth:rows, 0:width]
            second_ref[at + half : at + depth, :] = block[depth:rows, width : 2 * width]


def stack_either(core_ref, zero_ref, one_ref, first_ref, second_ref):
    @pl.when(core_ref[0] == 0)
    def _():
        stack(zero_ref, one_ref, first_ref, second_ref)

    @pl.when(core_ref[0] != 0)
    def _():
        stack(one_ref, zero_ref, first_ref, second_ref)


def expert_kernel(core_ref, slots_ref, zero_ref, one_ref, out_ref, first_ref, second_ref):
    width = second_ref.shape[1]
    stack_either(core_ref, zero_ref, one_ref, first_ref, second_ref)
    slots = slots_ref[...].reshape(out_ref.shape[0] * out_ref.shape[1], out_ref.shape[2])
    both = jnp.dot(slots, first_ref[...], preferred_element_type=F32)
    gate = both[:, 0:width]
    up = both[:, width : 2 * width]
    hidden = (gate * jax.nn.sigmoid(gate) * up).astype(BF)
    out = lax.dot_general(hidden, second_ref[...], NT, preferred_element_type=F32)
    out_ref[...] = out.astype(BF).reshape(out_ref.shape)


def whole_spec(shape):
    zeros = (0,) * len(shape)
    return pl.BlockSpec(shape, lambda i, *_: zeros)


def expert(core, slots, zero, one):
    width = zero.shape[2]
    grid_spec = pltpu.PrefetchScalarGridSpec(
        num_scalar_prefetch=1,
        grid=(1,),
        in_specs=[whole_spec(slots.shape), whole_spec(zero.shape), whole_spec(one.shape)],
        out_specs=whole_spec(slots.shape),
        scratch_shapes=[pltpu.VMEM((D, width), BF), pltpu.VMEM((D, width // 2), BF)],
    )
    return pl.pallas_call(
        expert_kernel,
        grid_spec=grid_spec,
        out_shape=jax.ShapeDtypeStruct(slots.shape, BF),
        compiler_params=PARAMS,
        name="expert",
    )(core, slots, zero, one)


def owner_kernel(core_ref, zero_ref, one_ref, gate_ref, up_ref, down_ref, first_ref, second_ref):
    width = second_ref.shape[1]
    stack_either(core_ref, zero_ref, one_ref, first_ref, second_ref)
    row = lax.broadcasted_iota(jnp.int32, (width, 2 * width), 0)
    lane = lax.broadcasted_iota(jnp.int32, (width, 2 * width), 1)
    first = first_ref[...]
    pick = (row == lane).astype(BF)
    gate_ref[...] = lax.dot_general(pick, first, NT, preferred_element_type=F32).astype(BF)
    pick = (row + width == lane).astype(BF)
    up_ref[...] = lax.dot_general(pick, first, NT, preferred_element_type=F32).astype(BF)
    row = lax.broadcasted_iota(jnp.int32, (width, width), 0)
    lane = lax.broadcasted_iota(jnp.int32, (width, width), 1)
    pick = (row == lane).astype(BF)
    down_ref[...] = lax.dot_general(pick, second_ref[...], NT, preferred_element_type=F32).astype(BF)


def owner(core, zero, one):
    width = zero.shape[2]
    shape = jax.ShapeDtypeStruct((width // 2, D), BF)
    grid_spec = pltpu.PrefetchScalarGridSpec(
        num_scalar_prefetch=1,
        grid=(1,),
        in_specs=[whole_spec(zero.shape), whole_spec(one.shape)],
        out_specs=[whole_spec(shape.shape)] * 3,
        scratch_shapes=[pltpu.VMEM((D, width), BF), pltpu.VMEM((D, width // 2), BF)],
    )
    return pl.pallas_call(
        owner_kernel,
        grid_spec=grid_spec,
        out_shape=(shape, shape, shape),
        compiler_params=PARAMS,
        name="owner",
    )(core, zero, one)


def along_z(hi, core):
    shape = (4, 2, 4, 2, 4)
    pairs = []
    for zh, co, x, zl, y in np.ndindex(shape):
        target = ((zh + hi) % 4, (zl + core) % 2, x, co, y)
        pairs.append((int(np.ravel_multi_index((zh, co, x, zl, y), shape)), int(np.ravel_multi_index(target, shape))))
    return pairs


def shards(
    queries,
    k_cache,
    v_cache,
    lengths,
    w_out,
    norm_gain,
    w_gate,
    w_up,
    w_down,
    expert_ids,
    gate_weights,
):
    cache_count = lax.axis_size(CACHE)
    cache_place = lax.axis_index(CACHE)
    step_count = queries.shape[0]
    row_count, positions = k_cache.shape[0], k_cache.shape[1]
    group_size = QH // KVH

    zh, core, zl = lax.axis_index("zh"), lax.axis_index("core"), lax.axis_index("zl")
    places = [(zh + hi) % 4 * 2 + (zl + c) % 2 for c in range(2) for hi in HI_STEPS]
    packed = pack(
        jnp.stack(places).astype(jnp.int32),
        jnp.transpose(w_gate, (1, 0, 2)),
        jnp.transpose(w_up, (1, 0, 2)),
        jnp.transpose(w_down, (2, 0, 1)),
    )
    packed, queries = lax.optimization_barrier((packed, queries))
    moved = [
        lax.ppermute(packed[c * 4 + i], CACHE + EXPERT, along_z(hi, c))
        for c in range(2)
        for i, hi in enumerate(HI_STEPS)
    ]

    query = queries.reshape(step_count, row_count, KVH, group_size, HD)
    query = jnp.transpose(query, (1, 0, 2, 3, 4))
    eye = jnp.eye(KVH, dtype=BF)
    query = query[:, :, :, :, None, :] * eye[None, None, :, None, :, None]
    query = query.reshape(row_count, step_count * QH, KVH * HD)
    base = (cache_place * positions).astype(jnp.int32).reshape(1)
    part = attend(lengths, base, query, k_cache, v_cache)
    parts = lax.all_gather(part, CACHE, axis=0)
    parts, moved[0:3] = lax.optimization_barrier((parts, moved[0:3]))
    own_heads = QH // cache_count
    parts = parts.reshape(cache_count, row_count, step_count, QH, 2 * HD)
    parts = lax.dynamic_slice_in_dim(parts, cache_place * own_heads, own_heads, 3).astype(F32)
    part_high = parts[..., HD : HD + 1]
    part_mass = parts[..., HD + 1 : HD + 2] + parts[..., HD + 2 : HD + 3]
    factor = jnp.exp(part_high - jnp.max(part_high, axis=0))
    own_out = jnp.sum(parts[..., 0:HD] * factor, axis=0) / jnp.sum(part_mass * factor, axis=0)
    own_rows = jnp.transpose(own_out.astype(BF), (1, 0, 2, 3)).reshape(step_count * row_count, own_heads * HD)
    projected = jnp.dot(own_rows, w_out, preferred_element_type=F32).astype(BF)
    projected = lax.all_gather(projected, CACHE, axis=0)
    projected, moved[3:5] = lax.optimization_barrier((projected, moved[3:5]))
    attention = jnp.sum(projected.astype(F32), axis=0)
    scale = lax.rsqrt(jnp.mean(attention * attention, axis=-1, keepdims=True) + 1e-05)
    normed = (attention * scale * norm_gain).astype(BF).reshape(step_count, row_count, D)

    experts_total = w_gate.shape[0] * cache_count
    capacity = max(2, (row_count * TOP + experts_total - 1) // experts_total)
    expert_range = jnp.arange(experts_total, dtype=jnp.int32)
    onehot = (expert_ids[..., None] == expert_range).astype(F32)
    chosen = jnp.sum(onehot, axis=2)
    gate_map = jnp.sum(onehot * gate_weights[..., None], axis=2)
    earlier = jnp.tril(jnp.ones((row_count, row_count), F32), -1)
    ranks = jnp.einsum("rq,sqe->sre", earlier, chosen, precision=lax.Precision.HIGHEST)
    slot_table = (ranks[..., None] == jnp.arange(capacity, dtype=F32)).astype(F32) * chosen[..., None]
    outgoing = jnp.einsum("srec,srd->escd", slot_table.astype(BF), normed, preferred_element_type=F32)
    outgoing = outgoing.astype(BF).reshape(experts_total, step_count * capacity, D)
    slots = lax.all_to_all(outgoing, EXPERT, split_axis=0, concat_axis=0, tiled=True)

    turns = jnp.stack([(zh - hi) % 4 for hi in HI_STEPS]).astype(jnp.int32)
    zero = join(turns, moved[0:4])
    zero, slots, moved[5:7] = lax.optimization_barrier((zero, slots, moved[5:7]))
    zero = lax.all_to_all(zero, ("x", "y"), split_axis=0, concat_axis=0, tiled=True)
    one = lax.all_to_all(join(turns, moved[4:8]), ("x", "y"), split_axis=0, concat_axis=0, tiled=True)
    core = core.astype(jnp.int32).reshape(1)
    partial_out = expert(core, slots, zero, one)
    returned = lax.all_to_all(partial_out, EXPERT, split_axis=0, concat_axis=0, tiled=True)
    zero, one, partial_out = lax.optimization_barrier((zero, one, partial_out))
    gate_owner, up_owner, down_owner = owner(core, zero, one)

    returned = returned.reshape(experts_total, step_count, capacity, D)
    combined = jnp.einsum(
        "srec,escd->srd",
        slot_table * gate_map[..., None],
        returned.astype(F32),
        precision=lax.Precision.HIGHEST,
    )
    shares = lax.all_gather(combined.astype(BF), CACHE, axis=0)
    total = jnp.sum(shares.astype(F32), axis=0) + attention.reshape(step_count, row_count, D)
    mixed = total.astype(BF)
    return (mixed, gate_owner.T[None], up_owner.T[None], down_owner[None])


def solution(mesh):
    return jax.shard_map(
        shards,
        mesh=Mesh(mesh.devices.reshape(4, 2, 4, 2, 4), CACHE + EXPERT),
        in_specs=(
            P(None, EXPERT, None),
            P(EXPERT, CACHE, None),
            P(EXPERT, CACHE, None),
            P(EXPERT),
            P(CACHE, None),
            P(),
            P(CACHE, EXPERT, None),
            P(CACHE, EXPERT, None),
            P(CACHE, None, EXPERT),
            P(None, EXPERT, None),
            P(None, EXPERT, None),
        ),
        out_specs=(
            P(None, EXPERT, None),
            P(EXPERT, None, CACHE),
            P(EXPERT, None, CACHE),
            P(EXPERT, CACHE, None),
        ),
        check_vma=False,
    )
```

```python
import math

import jax
import jax.numpy as jnp
import numpy as np
from jax import lax
from jax.experimental import pallas as pl
from jax.experimental.pallas import tpu as pltpu
from jax.sharding import Mesh
from jax.sharding import PartitionSpec as P

D = 2880
QH = 32
KVH = 4
HD = 64
TOP = 4
NEG = -1e30
BF = jnp.bfloat16
F32 = jnp.float32
NT = (((1,), (1,)), ((), ()))
CACHE = ("zh", "core")
EXPERT = ("x", "zl", "y")
HOPS = 4
CORES = 2
ROWS = 136
PIECES = ((2, 0, 136), (0, 0, 136), (1, 0, 136), (3, 0, 136))


def params(mib):
    return pltpu.CompilerParams(vmem_limit_bytes=mib << 20)


def pack_kernel(place_ref, gate_ref, up_ref, down_ref, *refs):
    out_refs, block_ref, sems = refs[:-2], refs[-2], refs[-1]
    blocks, experts = block_ref.shape[0], block_ref.shape[1]
    depth = gate_ref.shape[0]
    half = depth // 2
    width = gate_ref.shape[2] // blocks
    for k in range(experts):
        gate = gate_ref[:, k, :]
        up = up_ref[:, k, :]
        down = down_ref[:, k, :]
        for c in range(blocks):
            cut = slice(c * width, (c + 1) * width)
            block_ref[c, k, 0:depth, :] = jnp.concatenate([gate[:, cut], up[:, cut]], axis=1)
            block_ref[c, k, depth : depth + half, :] = jnp.concatenate(
                [down[0:half, cut], down[half:depth, cut]], axis=1
            )
    copies = [
        pltpu.make_async_copy(
            block_ref.at[pl.ds(place_ref[i] * CORES, CORES), :, start : start + size], out_refs[i], sems.at[i]
        )
        for i, (_, start, size) in enumerate(PIECES)
    ]
    for copy in copies:
        copy.start()
    for copy in copies:
        copy.wait()


def pack(places, gate, up, down):
    depth, experts, width = gate.shape
    blocks = HOPS * CORES
    columns = 2 * width // blocks
    whole = whole_spec(gate.shape)
    outs = [jax.ShapeDtypeStruct((CORES, experts, size, columns), BF) for _, _, size in PIECES]
    grid_spec = pltpu.PrefetchScalarGridSpec(
        num_scalar_prefetch=1,
        grid=(1,),
        in_specs=[whole, whole, whole],
        out_specs=[pl.BlockSpec(memory_space=pltpu.HBM)] * len(outs),
        scratch_shapes=[
            pltpu.VMEM((blocks, experts, ROWS, columns), BF),
            pltpu.SemaphoreType.DMA((len(outs),)),
        ],
    )
    return pl.pallas_call(
        pack_kernel,
        grid_spec=grid_spec,
        out_shape=outs,
        compiler_params=params(24),
        name="pack",
    )(places, gate, up, down)


def join_kernel(place_ref, *refs):
    in_refs, out_ref, sems = refs[:-2], refs[-2], refs[-1]
    copies = [
        pltpu.make_async_copy(in_ref, out_ref.at[:, place_ref[i], :, start : start + size], sems.at[i])
        for i, (in_ref, (_, start, size)) in enumerate(zip(in_refs, PIECES))
    ]
    for copy in copies:
        copy.start()
    for copy in copies:
        copy.wait()


def join(places, pieces):
    _, experts, _, columns = pieces[0].shape
    grid_spec = pltpu.PrefetchScalarGridSpec(
        num_scalar_prefetch=1,
        grid=(1,),
        in_specs=[pl.BlockSpec(memory_space=pl.ANY)] * len(pieces),
        out_specs=pl.BlockSpec(memory_space=pl.ANY),
        scratch_shapes=[pltpu.SemaphoreType.DMA((len(pieces),))],
    )
    joined = pl.pallas_call(
        join_kernel,
        grid_spec=grid_spec,
        out_shape=jax.ShapeDtypeStruct((CORES, HOPS, experts, ROWS, columns), BF),
        compiler_params=params(8),
        name="join",
    )(places, *pieces)
    return joined.reshape(CORES * HOPS * experts, ROWS, columns)


def attend_kernel(length_ref, base_ref, query_ref, key_ref, value_ref, out_ref):
    row = pl.program_id(0)
    heads = query_ref.shape[1]
    positions = key_ref.shape[1]
    scores = lax.dot_general(query_ref[0], key_ref[0], NT, preferred_element_type=F32)
    scores = scores * (1.0 / math.sqrt(HD))
    position = base_ref[0] + lax.broadcasted_iota(jnp.int32, (heads, positions), 1)
    step = (lax.broadcasted_iota(jnp.int32, (heads, positions), 0) >= heads // 2).astype(jnp.int32)
    visible = position < length_ref[row] + 1 + step
    highest = jnp.max(jnp.where(visible, scores, NEG), axis=-1, keepdims=True)
    highest = highest.astype(BF).astype(F32)
    weights = jnp.where(visible, jnp.exp(scores - highest), 0.0)
    mass = jnp.sum(weights, axis=-1, keepdims=True)
    wide = jnp.dot(weights.astype(BF), value_ref[0], preferred_element_type=F32)
    group = heads // (2 * KVH)
    own = (lax.broadcasted_iota(jnp.int32, (heads, HD), 0) // group) % KVH
    accum = jnp.zeros((heads, HD), F32)
    for h in range(KVH):
        accum = accum + jnp.where(own == h, wide[:, h * HD : (h + 1) * HD], 0.0)
    lane = lax.broadcasted_iota(jnp.int32, (heads, HD), 1)
    extra = jnp.where(lane == 0, highest, jnp.where(lane == 1, mass, 0.0))
    result = jnp.concatenate([accum, extra], axis=1)
    count = out_ref.shape[0]
    per = heads // (2 * count)
    for c in range(count):
        out_ref[c, 0] = jnp.concatenate(
            [result[c * per : (c + 1) * per], result[heads // 2 + c * per : heads // 2 + (c + 1) * per]], axis=0
        )


def attend(lengths, base, query, keys, values, count):
    rows, heads, width = query.shape
    positions = keys.shape[1]
    grid_spec = pltpu.PrefetchScalarGridSpec(
        num_scalar_prefetch=2,
        grid=(rows,),
        in_specs=[
            pl.BlockSpec((1, heads, width), lambda r, *_: (r, 0, 0)),
            pl.BlockSpec((1, positions, width), lambda r, *_: (r, 0, 0)),
            pl.BlockSpec((1, positions, width), lambda r, *_: (r, 0, 0)),
        ],
        out_specs=pl.BlockSpec((count, 1, heads // count, 2 * HD), lambda r, *_: (0, r, 0, 0)),
    )
    return pl.pallas_call(
        attend_kernel,
        grid_spec=grid_spec,
        out_shape=jax.ShapeDtypeStruct((count, rows, heads // count, 2 * HD), F32),
        compiler_params=params(12),
        name="attend",
    )(lengths, base, query, keys, values)


def stack(weights_ref, first_ref, second_ref):
    sources = weights_ref.shape[0]
    width = second_ref.shape[1]
    depth = first_ref.shape[0] // sources
    half = depth // 2
    per = sources // (CORES * HOPS)
    for i in range(sources):
        core, x, y = i // (HOPS * per), i // per % HOPS, i % per
        at = ((x * CORES + core) * per + y) * depth
        block = weights_ref[i]
        first_ref[at : at + depth, :] = block[0:depth]
        second_ref[at : at + half, :] = block[depth : depth + half, 0:width]
        second_ref[at + half : at + depth, :] = block[depth : depth + half, width : 2 * width]


def expert_kernel(slots_ref, weights_ref, out_ref, first_ref, second_ref):
    width = second_ref.shape[1]
    stack(weights_ref, first_ref, second_ref)
    slots = slots_ref[...].reshape(out_ref.shape[0] * out_ref.shape[1], out_ref.shape[2])
    both = jnp.dot(slots, first_ref[...], preferred_element_type=F32)
    gate = both[:, 0:width]
    up = both[:, width : 2 * width]
    hidden = (gate * jax.nn.sigmoid(gate) * up).astype(BF)
    out = lax.dot_general(hidden, second_ref[...], NT, preferred_element_type=F32)
    out_ref[...] = out.astype(BF).reshape(out_ref.shape)


def whole_spec(shape):
    zeros = (0,) * len(shape)
    return pl.BlockSpec(shape, lambda i, *_: zeros)


def expert(slots, weights):
    width = weights.shape[2]
    return pl.pallas_call(
        expert_kernel,
        out_shape=jax.ShapeDtypeStruct(slots.shape, BF),
        scratch_shapes=[pltpu.VMEM((D, width), BF), pltpu.VMEM((D, width // 2), BF)],
        compiler_params=params(28),
        name="expert",
    )(slots, weights)


def owner_kernel(weights_ref, gate_ref, up_ref, down_ref, first_ref, second_ref):
    width = second_ref.shape[1]
    stack(weights_ref, first_ref, second_ref)
    row = lax.broadcasted_iota(jnp.int32, (width, 2 * width), 0)
    lane = lax.broadcasted_iota(jnp.int32, (width, 2 * width), 1)
    first = first_ref[...]
    pick = (row == lane).astype(BF)
    gate_ref[...] = lax.dot_general(pick, first, NT, preferred_element_type=F32).astype(BF)
    pick = (row + width == lane).astype(BF)
    up_ref[...] = lax.dot_general(pick, first, NT, preferred_element_type=F32).astype(BF)
    row = lax.broadcasted_iota(jnp.int32, (width, width), 0)
    lane = lax.broadcasted_iota(jnp.int32, (width, width), 1)
    pick = (row == lane).astype(BF)
    down_ref[...] = lax.dot_general(pick, second_ref[...], NT, preferred_element_type=F32).astype(BF)


def owner(weights):
    width = weights.shape[2]
    shape = jax.ShapeDtypeStruct((width // 2, D), BF)
    return pl.pallas_call(
        owner_kernel,
        out_shape=(shape, shape, shape),
        scratch_shapes=[pltpu.VMEM((D, width), BF), pltpu.VMEM((D, width // 2), BF)],
        compiler_params=params(28),
        name="owner",
    )(weights)


def along_z(hi):
    shape = (4, 2, 4, 2, 4)
    pairs = []
    for zh, core, x, zl, y in np.ndindex(shape):
        target = ((zh + hi) % 4, zl, x, core, y)
        pairs.append((int(np.ravel_multi_index((zh, core, x, zl, y), shape)), int(np.ravel_multi_index(target, shape))))
    return pairs


def shards(
    queries,
    k_cache,
    v_cache,
    lengths,
    w_out,
    norm_gain,
    w_gate,
    w_up,
    w_down,
    expert_ids,
    gate_weights,
):
    cache_count = lax.axis_size(CACHE)
    cache_place = lax.axis_index(CACHE)
    step_count = queries.shape[0]
    row_count, positions = k_cache.shape[0], k_cache.shape[1]
    group_size = QH // KVH

    zh = lax.axis_index("zh")
    packed = pack(
        jnp.stack([(zh + hi) % HOPS for hi, _, _ in PIECES]).astype(jnp.int32),
        jnp.transpose(w_gate, (1, 0, 2)),
        jnp.transpose(w_up, (1, 0, 2)),
        jnp.transpose(w_down, (2, 0, 1)),
    )
    packed, queries = lax.optimization_barrier((packed, queries))
    moved = [lax.ppermute(block, CACHE + EXPERT, along_z(piece[0])) for block, piece in zip(packed, PIECES)]

    query = queries.reshape(step_count, row_count, KVH, group_size, HD)
    query = jnp.transpose(query, (1, 0, 2, 3, 4))
    eye = jnp.eye(KVH, dtype=BF)
    query = query[:, :, :, :, None, :] * eye[None, None, :, None, :, None]
    query = query.reshape(row_count, step_count * QH, KVH * HD)
    base = (cache_place * positions).astype(jnp.int32).reshape(1)
    part = attend(lengths, base, query, k_cache, v_cache, cache_count)
    parts = lax.all_to_all(part, CACHE, split_axis=0, concat_axis=0, tiled=True)
    parts, moved[:2] = lax.optimization_barrier((parts, moved[:2]))

    own_heads = QH // cache_count
    parts = parts.reshape(cache_count, row_count, step_count, own_heads, 2 * HD)
    part_high = parts[..., HD : HD + 1]
    part_mass = parts[..., HD + 1 : HD + 2]
    factor = jnp.exp(part_high - jnp.max(part_high, axis=0))
    own_out = jnp.sum(parts[..., 0:HD] * factor, axis=0) / jnp.sum(part_mass * factor, axis=0)
    own_rows = jnp.transpose(own_out.astype(BF), (1, 0, 2, 3)).reshape(step_count * row_count, own_heads * HD)
    projected = jnp.dot(own_rows, w_out, preferred_element_type=F32).astype(BF)
    projected = jnp.broadcast_to(projected[None], (cache_count, *projected.shape))
    projected = lax.all_to_all(projected, CACHE, split_axis=0, concat_axis=0, tiled=True)
    projected, moved[2:4] = lax.optimization_barrier((projected, moved[2:4]))
    attention = jnp.sum(projected.astype(F32), axis=0)
    scale = lax.rsqrt(jnp.mean(attention * attention, axis=-1, keepdims=True) + 1e-05)
    normed = (attention * scale * norm_gain).astype(BF).reshape(step_count, row_count, D)

    experts_total = w_gate.shape[0] * cache_count
    capacity = max(2, (row_count * TOP + experts_total - 1) // experts_total)
    expert_range = jnp.arange(experts_total, dtype=jnp.int32)
    onehot = (expert_ids[..., None] == expert_range).astype(F32)
    chosen = jnp.sum(onehot, axis=2)
    gate_map = jnp.sum(onehot * gate_weights[..., None], axis=2)
    earlier = jnp.tril(jnp.ones((row_count, row_count), F32), -1)
    ranks = jnp.einsum("rq,sqe->sre", earlier, chosen, precision=lax.Precision.HIGHEST)
    slot_table = (ranks[..., None] == jnp.arange(capacity, dtype=F32)).astype(F32) * chosen[..., None]
    outgoing = jnp.einsum("srec,srd->escd", slot_table.astype(BF), normed, preferred_element_type=F32)
    outgoing = outgoing.astype(BF).reshape(experts_total, step_count * capacity, D)
    slots = lax.all_to_all(outgoing, EXPERT, split_axis=0, concat_axis=0, tiled=True)

    turns = jnp.stack([(zh - hi) % HOPS for hi, _, _ in PIECES]).astype(jnp.int32)
    slots, moved = lax.optimization_barrier((slots, moved))
    arrived = lax.all_to_all(join(turns, moved), ("core", "x", "y"), split_axis=0, concat_axis=0, tiled=True)
    partial_out = expert(slots, arrived)
    returned = lax.all_to_all(partial_out, EXPERT, split_axis=0, concat_axis=0, tiled=True)
    arrived, partial_out = lax.optimization_barrier((arrived, partial_out))
    gate_owner, up_owner, down_owner = owner(arrived)

    returned = returned.reshape(experts_total, step_count, capacity, D)
    combined = jnp.einsum(
        "srec,escd->srd",
        slot_table * gate_map[..., None],
        returned.astype(F32),
        precision=lax.Precision.HIGHEST,
    )
    shares = lax.all_gather(combined.astype(BF), CACHE, axis=0)
    total = jnp.sum(shares.astype(F32), axis=0) + attention.reshape(step_count, row_count, D)
    mixed = total.astype(BF)
    return (mixed, gate_owner.T[None], up_owner.T[None], down_owner[None])


def solution(mesh):
    return jax.shard_map(
        shards,
        mesh=Mesh(mesh.devices.reshape(4, 2, 4, 2, 4), CACHE + EXPERT),
        in_specs=(
            P(None, EXPERT, None),
            P(EXPERT, CACHE, None),
            P(EXPERT, CACHE, None),
            P(EXPERT),
            P(CACHE, None),
            P(),
            P(CACHE, EXPERT, None),
            P(CACHE, EXPERT, None),
            P(CACHE, None, EXPERT),
            P(None, EXPERT, None),
            P(None, EXPERT, None),
        ),
        out_specs=(
            P(None, EXPERT, None),
            P(EXPERT, None, CACHE),
            P(EXPERT, None, CACHE),
            P(EXPERT, CACHE, None),
        ),
        check_vma=False,
    )
```

```python
import math

import jax
import jax.numpy as jnp
import numpy as np
from jax import lax
from jax.experimental import pallas as pl
from jax.experimental.pallas import tpu as pltpu
from jax.sharding import Mesh
from jax.sharding import PartitionSpec as P

D = 2880
QH = 32
KVH = 4
HD = 64
TOP = 4
NEG = -1e30
BF = jnp.bfloat16
F32 = jnp.float32
NT = (((1,), (1,)), ((), ()))
CACHE = ("zh", "core")
EXPERT = ("x", "zl", "y")
HOPS = 4
CORES = 2
ROWS = 136
PIECES = ((2, 0, 136), (0, 0, 136), (1, 0, 136), (3, 0, 136))


def params(mib):
    return pltpu.CompilerParams(vmem_limit_bytes=mib << 20)


def pack_kernel(place_ref, gate_ref, up_ref, down_ref, *refs):
    out_refs, block_ref, sems = refs[:-2], refs[-2], refs[-1]
    blocks, experts = block_ref.shape[0], block_ref.shape[1]
    depth = gate_ref.shape[0]
    half = depth // 2
    width = gate_ref.shape[2] // blocks
    for k in range(experts):
        gate = gate_ref[:, k, :]
        up = up_ref[:, k, :]
        down = down_ref[:, k, :]
        for c in range(blocks):
            cut = slice(c * width, (c + 1) * width)
            block_ref[c, k, 0:depth, :] = jnp.concatenate([gate[:, cut], up[:, cut]], axis=1)
            block_ref[c, k, depth : depth + half, :] = jnp.concatenate(
                [down[0:half, cut], down[half:depth, cut]], axis=1
            )
    copies = [
        pltpu.make_async_copy(
            block_ref.at[pl.ds(place_ref[i] * CORES, CORES), :, start : start + size], out_refs[i], sems.at[i]
        )
        for i, (_, start, size) in enumerate(PIECES)
    ]
    for copy in copies:
        copy.start()
    for copy in copies:
        copy.wait()


def pack(places, gate, up, down):
    depth, experts, width = gate.shape
    blocks = HOPS * CORES
    columns = 2 * width // blocks
    whole = whole_spec(gate.shape)
    outs = [jax.ShapeDtypeStruct((CORES, experts, size, columns), BF) for _, _, size in PIECES]
    grid_spec = pltpu.PrefetchScalarGridSpec(
        num_scalar_prefetch=1,
        grid=(1,),
        in_specs=[whole, whole, whole],
        out_specs=[pl.BlockSpec(memory_space=pltpu.HBM)] * len(outs),
        scratch_shapes=[
            pltpu.VMEM((blocks, experts, ROWS, columns), BF),
            pltpu.SemaphoreType.DMA((len(outs),)),
        ],
    )
    return pl.pallas_call(
        pack_kernel,
        grid_spec=grid_spec,
        out_shape=outs,
        compiler_params=params(24),
        name="pack",
    )(places, gate, up, down)


def join_kernel(place_ref, *refs):
    in_refs, out_ref, sems = refs[:-2], refs[-2], refs[-1]
    copies = [
        pltpu.make_async_copy(in_ref, out_ref.at[:, place_ref[i], :, start : start + size], sems.at[i])
        for i, (in_ref, (_, start, size)) in enumerate(zip(in_refs, PIECES))
    ]
    for copy in copies:
        copy.start()
    for copy in copies:
        copy.wait()


def join(places, pieces):
    _, experts, _, columns = pieces[0].shape
    grid_spec = pltpu.PrefetchScalarGridSpec(
        num_scalar_prefetch=1,
        grid=(1,),
        in_specs=[pl.BlockSpec(memory_space=pl.ANY)] * len(pieces),
        out_specs=pl.BlockSpec(memory_space=pl.ANY),
        scratch_shapes=[pltpu.SemaphoreType.DMA((len(pieces),))],
    )
    joined = pl.pallas_call(
        join_kernel,
        grid_spec=grid_spec,
        out_shape=jax.ShapeDtypeStruct((CORES, HOPS, experts, ROWS, columns), BF),
        compiler_params=params(8),
        name="join",
    )(places, *pieces)
    return joined.reshape(CORES * HOPS * experts, ROWS, columns)


def attend_kernel(length_ref, base_ref, query_ref, key_ref, value_ref, out_ref):
    row = pl.program_id(0)
    heads = query_ref.shape[1]
    positions = key_ref.shape[1]
    scores = lax.dot_general(query_ref[0], key_ref[0], NT, preferred_element_type=F32)
    scores = scores * (1.0 / math.sqrt(HD))
    position = base_ref[0] + lax.broadcasted_iota(jnp.int32, (heads, positions), 1)
    step = (lax.broadcasted_iota(jnp.int32, (heads, positions), 0) >= heads // 2).astype(jnp.int32)
    visible = position < length_ref[row] + 1 + step
    highest = jnp.max(jnp.where(visible, scores, NEG), axis=-1, keepdims=True)
    highest = highest.astype(BF).astype(F32)
    weights = jnp.where(visible, jnp.exp(scores - highest), 0.0)
    mass = jnp.sum(weights, axis=-1, keepdims=True)
    wide = jnp.dot(weights.astype(BF), value_ref[0], preferred_element_type=F32)
    group = heads // (2 * KVH)
    own = (lax.broadcasted_iota(jnp.int32, (heads, HD), 0) // group) % KVH
    accum = jnp.zeros((heads, HD), F32)
    for h in range(KVH):
        accum = accum + jnp.where(own == h, wide[:, h * HD : (h + 1) * HD], 0.0)
    lane = lax.broadcasted_iota(jnp.int32, (heads, HD), 1)
    extra = jnp.where(lane == 0, highest, jnp.where(lane == 1, mass, 0.0))
    result = jnp.concatenate([accum, extra], axis=1)
    count = out_ref.shape[0]
    per = heads // (2 * count)
    for c in range(count):
        out_ref[c, 0] = jnp.concatenate(
            [result[c * per : (c + 1) * per], result[heads // 2 + c * per : heads // 2 + (c + 1) * per]], axis=0
        )


def attend(lengths, base, query, keys, values, count):
    rows, heads, width = query.shape
    positions = keys.shape[1]
    grid_spec = pltpu.PrefetchScalarGridSpec(
        num_scalar_prefetch=2,
        grid=(rows,),
        in_specs=[
            pl.BlockSpec((1, heads, width), lambda r, *_: (r, 0, 0)),
            pl.BlockSpec((1, positions, width), lambda r, *_: (r, 0, 0)),
            pl.BlockSpec((1, positions, width), lambda r, *_: (r, 0, 0)),
        ],
        out_specs=pl.BlockSpec((count, 1, heads // count, 2 * HD), lambda r, *_: (0, r, 0, 0)),
    )
    return pl.pallas_call(
        attend_kernel,
        grid_spec=grid_spec,
        out_shape=jax.ShapeDtypeStruct((count, rows, heads // count, 2 * HD), F32),
        compiler_params=params(12),
        name="attend",
    )(lengths, base, query, keys, values)


def stack(weights_ref, first_ref, second_ref):
    sources = weights_ref.shape[0]
    width = second_ref.shape[1]
    depth = first_ref.shape[0] // sources
    half = depth // 2
    per = sources // (CORES * HOPS)
    for i in range(sources):
        core, x, y = i // (HOPS * per), i // per % HOPS, i % per
        at = ((x * CORES + core) * per + y) * depth
        block = weights_ref[i]
        first_ref[at : at + depth, :] = block[0:depth]
        second_ref[at : at + half, :] = block[depth : depth + half, 0:width]
        second_ref[at + half : at + depth, :] = block[depth : depth + half, width : 2 * width]


def expert_kernel(slots_ref, weights_ref, out_ref, first_ref, second_ref):
    width = second_ref.shape[1]
    stack(weights_ref, first_ref, second_ref)
    slots = slots_ref[...].reshape(out_ref.shape[0] * out_ref.shape[1], out_ref.shape[2])
    both = jnp.dot(slots, first_ref[...], preferred_element_type=F32)
    gate = both[:, 0:width]
    up = both[:, width : 2 * width]
    hidden = (gate * jax.nn.sigmoid(gate) * up).astype(BF)
    out = lax.dot_general(hidden, second_ref[...], NT, preferred_element_type=F32)
    out_ref[...] = out.astype(BF).reshape(out_ref.shape)


def whole_spec(shape):
    zeros = (0,) * len(shape)
    return pl.BlockSpec(shape, lambda i, *_: zeros)


def expert(slots, weights):
    width = weights.shape[2]
    return pl.pallas_call(
        expert_kernel,
        out_shape=jax.ShapeDtypeStruct(slots.shape, BF),
        scratch_shapes=[pltpu.VMEM((D, width), BF), pltpu.VMEM((D, width // 2), BF)],
        compiler_params=params(28),
        name="expert",
    )(slots, weights)


def owner_kernel(weights_ref, gate_ref, up_ref, down_ref, first_ref, second_ref):
    width = second_ref.shape[1]
    stack(weights_ref, first_ref, second_ref)
    row = lax.broadcasted_iota(jnp.int32, (width, 2 * width), 0)
    lane = lax.broadcasted_iota(jnp.int32, (width, 2 * width), 1)
    first = first_ref[...]
    pick = (row == lane).astype(BF)
    gate_ref[...] = lax.dot_general(pick, first, NT, preferred_element_type=F32).astype(BF)
    pick = (row + width == lane).astype(BF)
    up_ref[...] = lax.dot_general(pick, first, NT, preferred_element_type=F32).astype(BF)
    row = lax.broadcasted_iota(jnp.int32, (width, width), 0)
    lane = lax.broadcasted_iota(jnp.int32, (width, width), 1)
    pick = (row == lane).astype(BF)
    down_ref[...] = lax.dot_general(pick, second_ref[...], NT, preferred_element_type=F32).astype(BF)


def owner(weights):
    width = weights.shape[2]
    shape = jax.ShapeDtypeStruct((width // 2, D), BF)
    return pl.pallas_call(
        owner_kernel,
        out_shape=(shape, shape, shape),
        scratch_shapes=[pltpu.VMEM((D, width), BF), pltpu.VMEM((D, width // 2), BF)],
        compiler_params=params(28),
        name="owner",
    )(weights)


def along_z(hi):
    shape = (4, 2, 4, 2, 4)
    pairs = []
    for zh, core, x, zl, y in np.ndindex(shape):
        target = ((zh + hi) % 4, zl, x, core, y)
        pairs.append((int(np.ravel_multi_index((zh, core, x, zl, y), shape)), int(np.ravel_multi_index(target, shape))))
    return pairs


def shards(
    queries,
    k_cache,
    v_cache,
    lengths,
    w_out,
    norm_gain,
    w_gate,
    w_up,
    w_down,
    expert_ids,
    gate_weights,
):
    cache_count = lax.axis_size(CACHE)
    cache_place = lax.axis_index(CACHE)
    step_count = queries.shape[0]
    row_count, positions = k_cache.shape[0], k_cache.shape[1]
    group_size = QH // KVH

    zh = lax.axis_index("zh")
    packed = pack(
        jnp.stack([(zh + hi) % HOPS for hi, _, _ in PIECES]).astype(jnp.int32),
        jnp.transpose(w_gate, (1, 0, 2)),
        jnp.transpose(w_up, (1, 0, 2)),
        jnp.transpose(w_down, (2, 0, 1)),
    )
    packed, queries = lax.optimization_barrier((packed, queries))
    moved = [lax.ppermute(block, CACHE + EXPERT, along_z(piece[0])) for block, piece in zip(packed, PIECES)]

    query = queries.reshape(step_count, row_count, KVH, group_size, HD)
    query = jnp.transpose(query, (1, 0, 2, 3, 4))
    eye = jnp.eye(KVH, dtype=BF)
    query = query[:, :, :, :, None, :] * eye[None, None, :, None, :, None]
    query = query.reshape(row_count, step_count * QH, KVH * HD)
    base = (cache_place * positions).astype(jnp.int32).reshape(1)
    part = attend(lengths, base, query, k_cache, v_cache, cache_count)
    parts = lax.all_to_all(part, CACHE, split_axis=0, concat_axis=0, tiled=True)
    parts, moved[:2] = lax.optimization_barrier((parts, moved[:2]))

    own_heads = QH // cache_count
    parts = parts.reshape(cache_count, row_count, step_count, own_heads, 2 * HD)
    part_high = parts[..., HD : HD + 1]
    part_mass = parts[..., HD + 1 : HD + 2]
    factor = jnp.exp(part_high - jnp.max(part_high, axis=0))
    own_out = jnp.sum(parts[..., 0:HD] * factor, axis=0) / jnp.sum(part_mass * factor, axis=0)
    own_rows = jnp.transpose(own_out.astype(BF), (1, 0, 2, 3)).reshape(step_count * row_count, own_heads * HD)
    projected = jnp.dot(own_rows, w_out, preferred_element_type=F32).astype(BF)
    projected = jnp.broadcast_to(projected[None], (cache_count, *projected.shape))
    projected = lax.all_to_all(projected, CACHE, split_axis=0, concat_axis=0, tiled=True)
    projected, moved[2:4] = lax.optimization_barrier((projected, moved[2:4]))
    attention = jnp.sum(projected.astype(F32), axis=0)
    scale = lax.rsqrt(jnp.mean(attention * attention, axis=-1, keepdims=True) + 1e-05)
    normed = (attention * scale * norm_gain).astype(BF).reshape(step_count, row_count, D)

    experts_total = w_gate.shape[0] * cache_count
    capacity = max(2, (row_count * TOP + experts_total - 1) // experts_total)
    expert_range = jnp.arange(experts_total, dtype=jnp.int32)
    onehot = (expert_ids[..., None] == expert_range).astype(F32)
    chosen = jnp.sum(onehot, axis=2)
    gate_map = jnp.sum(onehot * gate_weights[..., None], axis=2)
    earlier = jnp.tril(jnp.ones((row_count, row_count), F32), -1)
    ranks = jnp.einsum("rq,sqe->sre", earlier, chosen, precision=lax.Precision.HIGHEST)
    slot_table = (ranks[..., None] == jnp.arange(capacity, dtype=F32)).astype(F32) * chosen[..., None]
    outgoing = jnp.einsum("srec,srd->escd", slot_table.astype(BF), normed, preferred_element_type=F32)
    outgoing = outgoing.astype(BF).reshape(experts_total, step_count * capacity, D)
    slots = lax.all_to_all(outgoing, EXPERT, split_axis=0, concat_axis=0, tiled=True)

    turns = jnp.stack([(zh - hi) % HOPS for hi, _, _ in PIECES]).astype(jnp.int32)
    joined, slots = lax.optimization_barrier((join(turns, moved), slots))
    arrived = lax.all_to_all(joined, ("core", "x", "y"), split_axis=0, concat_axis=0, tiled=True)
    partial_out = expert(slots, arrived)
    returned = lax.all_to_all(partial_out, EXPERT, split_axis=0, concat_axis=0, tiled=True)
    arrived, partial_out = lax.optimization_barrier((arrived, partial_out))
    gate_owner, up_owner, down_owner = owner(arrived)

    returned = returned.reshape(experts_total, step_count, capacity, D)
    combined = jnp.einsum(
        "srec,escd->srd",
        slot_table * gate_map[..., None],
        returned.astype(F32),
        precision=lax.Precision.HIGHEST,
    )
    shares = lax.all_gather(combined.astype(BF), CACHE, axis=0)
    total = jnp.sum(shares.astype(F32), axis=0) + attention.reshape(step_count, row_count, D)
    mixed = total.astype(BF)
    return (mixed, gate_owner.T[None], up_owner.T[None], down_owner[None])


def solution(mesh):
    return jax.shard_map(
        shards,
        mesh=Mesh(mesh.devices.reshape(4, 2, 4, 2, 4), CACHE + EXPERT),
        in_specs=(
            P(None, EXPERT, None),
            P(EXPERT, CACHE, None),
            P(EXPERT, CACHE, None),
            P(EXPERT),
            P(CACHE, None),
            P(),
            P(CACHE, EXPERT, None),
            P(CACHE, EXPERT, None),
            P(CACHE, None, EXPERT),
            P(None, EXPERT, None),
            P(None, EXPERT, None),
        ),
        out_specs=(
            P(None, EXPERT, None),
            P(EXPERT, None, CACHE),
            P(EXPERT, None, CACHE),
            P(EXPERT, CACHE, None),
        ),
        check_vma=False,
    )
```

```python
import math

import jax
import jax.numpy as jnp
import numpy as np
from jax import lax
from jax.experimental import pallas as pl
from jax.experimental.pallas import tpu as pltpu
from jax.sharding import Mesh
from jax.sharding import PartitionSpec as P

D = 2880
QH = 32
KVH = 4
HD = 64
TOP = 4
NEG = -1e30
BF = jnp.bfloat16
F32 = jnp.float32
NT = (((1,), (1,)), ((), ()))
CACHE = ("zh", "core")
EXPERT = ("x", "zl", "y")
HOPS = 4
CORES = 2
ROWS = 136
PIECES = ((1, 0, 136), (3, 0, 136), (2, 0, 136), (0, 0, 136))


def params(mib):
    return pltpu.CompilerParams(vmem_limit_bytes=mib << 20)


def pack_kernel(place_ref, gate_ref, up_ref, down_ref, *refs):
    out_refs, block_ref, sems = refs[:-2], refs[-2], refs[-1]
    blocks, experts = block_ref.shape[0], block_ref.shape[1]
    depth = gate_ref.shape[0]
    half = depth // 2
    width = gate_ref.shape[2] // blocks
    for k in range(experts):
        gate = gate_ref[:, k, :]
        up = up_ref[:, k, :]
        down = down_ref[:, k, :]
        for c in range(blocks):
            cut = slice(c * width, (c + 1) * width)
            block_ref[c, k, 0:depth, :] = jnp.concatenate([gate[:, cut], up[:, cut]], axis=1)
            block_ref[c, k, depth : depth + half, :] = jnp.concatenate(
                [down[0:half, cut], down[half:depth, cut]], axis=1
            )
    copies = [
        pltpu.make_async_copy(
            block_ref.at[pl.ds(place_ref[i] * CORES, CORES), :, start : start + size], out_refs[i], sems.at[i]
        )
        for i, (_, start, size) in enumerate(PIECES)
    ]
    for copy in copies:
        copy.start()
    for copy in copies:
        copy.wait()


def pack(places, gate, up, down):
    depth, experts, width = gate.shape
    blocks = HOPS * CORES
    columns = 2 * width // blocks
    whole = whole_spec(gate.shape)
    outs = [jax.ShapeDtypeStruct((CORES, experts, size, columns), BF) for _, _, size in PIECES]
    grid_spec = pltpu.PrefetchScalarGridSpec(
        num_scalar_prefetch=1,
        grid=(1,),
        in_specs=[whole, whole, whole],
        out_specs=[pl.BlockSpec(memory_space=pltpu.HBM)] * len(outs),
        scratch_shapes=[
            pltpu.VMEM((blocks, experts, ROWS, columns), BF),
            pltpu.SemaphoreType.DMA((len(outs),)),
        ],
    )
    return pl.pallas_call(
        pack_kernel,
        grid_spec=grid_spec,
        out_shape=outs,
        compiler_params=params(24),
        name="pack",
    )(places, gate, up, down)


def join_kernel(place_ref, *refs):
    in_refs, out_ref, sems = refs[:-2], refs[-2], refs[-1]
    copies = [
        pltpu.make_async_copy(in_ref, out_ref.at[:, place_ref[i], :, start : start + size], sems.at[i])
        for i, (in_ref, (_, start, size)) in enumerate(zip(in_refs, PIECES))
    ]
    for copy in copies:
        copy.start()
    for copy in copies:
        copy.wait()


def join(places, pieces):
    _, experts, _, columns = pieces[0].shape
    grid_spec = pltpu.PrefetchScalarGridSpec(
        num_scalar_prefetch=1,
        grid=(1,),
        in_specs=[pl.BlockSpec(memory_space=pl.ANY)] * len(pieces),
        out_specs=pl.BlockSpec(memory_space=pl.ANY),
        scratch_shapes=[pltpu.SemaphoreType.DMA((len(pieces),))],
    )
    joined = pl.pallas_call(
        join_kernel,
        grid_spec=grid_spec,
        out_shape=jax.ShapeDtypeStruct((CORES, HOPS, experts, ROWS, columns), BF),
        compiler_params=params(8),
        name="join",
    )(places, *pieces)
    return joined.reshape(CORES * HOPS * experts, ROWS, columns)


def attend_kernel(length_ref, base_ref, query_ref, key_ref, value_ref, out_ref):
    row = pl.program_id(0)
    heads = query_ref.shape[1]
    positions = key_ref.shape[1]
    scores = lax.dot_general(query_ref[0], key_ref[0], NT, preferred_element_type=F32)
    scores = scores * (1.0 / math.sqrt(HD))
    position = base_ref[0] + lax.broadcasted_iota(jnp.int32, (heads, positions), 1)
    step = (lax.broadcasted_iota(jnp.int32, (heads, positions), 0) >= heads // 2).astype(jnp.int32)
    visible = position < length_ref[row] + 1 + step
    highest = jnp.max(jnp.where(visible, scores, NEG), axis=-1, keepdims=True)
    highest = highest.astype(BF).astype(F32)
    weights = jnp.where(visible, jnp.exp(scores - highest), 0.0)
    mass = jnp.sum(weights, axis=-1, keepdims=True)
    wide = jnp.dot(weights.astype(BF), value_ref[0], preferred_element_type=F32)
    group = heads // (2 * KVH)
    own = (lax.broadcasted_iota(jnp.int32, (heads, HD), 0) // group) % KVH
    accum = jnp.zeros((heads, HD), F32)
    for h in range(KVH):
        accum = accum + jnp.where(own == h, wide[:, h * HD : (h + 1) * HD], 0.0)
    lane = lax.broadcasted_iota(jnp.int32, (heads, HD), 1)
    extra = jnp.where(lane == 0, highest, jnp.where(lane == 1, mass, 0.0))
    result = jnp.concatenate([accum, extra], axis=1)
    count = out_ref.shape[0]
    per = heads // (2 * count)
    for c in range(count):
        out_ref[c, 0] = jnp.concatenate(
            [result[c * per : (c + 1) * per], result[heads // 2 + c * per : heads // 2 + (c + 1) * per]], axis=0
        )


def attend(lengths, base, query, keys, values, count):
    rows, heads, width = query.shape
    positions = keys.shape[1]
    grid_spec = pltpu.PrefetchScalarGridSpec(
        num_scalar_prefetch=2,
        grid=(rows,),
        in_specs=[
            pl.BlockSpec((1, heads, width), lambda r, *_: (r, 0, 0)),
            pl.BlockSpec((1, positions, width), lambda r, *_: (r, 0, 0)),
            pl.BlockSpec((1, positions, width), lambda r, *_: (r, 0, 0)),
        ],
        out_specs=pl.BlockSpec((count, 1, heads // count, 2 * HD), lambda r, *_: (0, r, 0, 0)),
    )
    return pl.pallas_call(
        attend_kernel,
        grid_spec=grid_spec,
        out_shape=jax.ShapeDtypeStruct((count, rows, heads // count, 2 * HD), F32),
        compiler_params=params(12),
        name="attend",
    )(lengths, base, query, keys, values)


def stack(weights_ref, first_ref, second_ref):
    sources = weights_ref.shape[0]
    width = second_ref.shape[1]
    depth = first_ref.shape[0] // sources
    half = depth // 2
    per = sources // (CORES * HOPS)
    for i in range(sources):
        core, x, y = i // (HOPS * per), i // per % HOPS, i % per
        at = ((x * CORES + core) * per + y) * depth
        block = weights_ref[i]
        first_ref[at : at + depth, :] = block[0:depth]
        second_ref[at : at + half, :] = block[depth : depth + half, 0:width]
        second_ref[at + half : at + depth, :] = block[depth : depth + half, width : 2 * width]


def expert_kernel(slots_ref, weights_ref, out_ref, first_ref, second_ref):
    width = second_ref.shape[1]
    stack(weights_ref, first_ref, second_ref)
    slots = slots_ref[...].reshape(out_ref.shape[0] * out_ref.shape[1], out_ref.shape[2])
    both = jnp.dot(slots, first_ref[...], preferred_element_type=F32)
    gate = both[:, 0:width]
    up = both[:, width : 2 * width]
    hidden = (gate * jax.nn.sigmoid(gate) * up).astype(BF)
    out = lax.dot_general(hidden, second_ref[...], NT, preferred_element_type=F32)
    out_ref[...] = out.astype(BF).reshape(out_ref.shape)


def whole_spec(shape):
    zeros = (0,) * len(shape)
    return pl.BlockSpec(shape, lambda i, *_: zeros)


def expert(slots, weights):
    width = weights.shape[2]
    return pl.pallas_call(
        expert_kernel,
        out_shape=jax.ShapeDtypeStruct(slots.shape, BF),
        scratch_shapes=[pltpu.VMEM((D, width), BF), pltpu.VMEM((D, width // 2), BF)],
        compiler_params=params(28),
        name="expert",
    )(slots, weights)


def owner_kernel(weights_ref, gate_ref, up_ref, down_ref, first_ref, second_ref):
    width = second_ref.shape[1]
    stack(weights_ref, first_ref, second_ref)
    row = lax.broadcasted_iota(jnp.int32, (width, 2 * width), 0)
    lane = lax.broadcasted_iota(jnp.int32, (width, 2 * width), 1)
    first = first_ref[...]
    pick = (row == lane).astype(BF)
    gate_ref[...] = lax.dot_general(pick, first, NT, preferred_element_type=F32).astype(BF)
    pick = (row + width == lane).astype(BF)
    up_ref[...] = lax.dot_general(pick, first, NT, preferred_element_type=F32).astype(BF)
    row = lax.broadcasted_iota(jnp.int32, (width, width), 0)
    lane = lax.broadcasted_iota(jnp.int32, (width, width), 1)
    pick = (row == lane).astype(BF)
    down_ref[...] = lax.dot_general(pick, second_ref[...], NT, preferred_element_type=F32).astype(BF)


def owner(weights):
    width = weights.shape[2]
    shape = jax.ShapeDtypeStruct((width // 2, D), BF)
    return pl.pallas_call(
        owner_kernel,
        out_shape=(shape, shape, shape),
        scratch_shapes=[pltpu.VMEM((D, width), BF), pltpu.VMEM((D, width // 2), BF)],
        compiler_params=params(28),
        name="owner",
    )(weights)


def along_z(hi):
    shape = (4, 2, 4, 2, 4)
    pairs = []
    for zh, core, x, zl, y in np.ndindex(shape):
        target = ((zh + hi) % 4, zl, x, core, y)
        pairs.append((int(np.ravel_multi_index((zh, core, x, zl, y), shape)), int(np.ravel_multi_index(target, shape))))
    return pairs


def shards(
    queries,
    k_cache,
    v_cache,
    lengths,
    w_out,
    norm_gain,
    w_gate,
    w_up,
    w_down,
    expert_ids,
    gate_weights,
):
    cache_count = lax.axis_size(CACHE)
    cache_place = lax.axis_index(CACHE)
    step_count = queries.shape[0]
    row_count, positions = k_cache.shape[0], k_cache.shape[1]
    group_size = QH // KVH

    zh = lax.axis_index("zh")
    packed = pack(
        jnp.stack([(zh + hi) % HOPS for hi, _, _ in PIECES]).astype(jnp.int32),
        jnp.transpose(w_gate, (1, 0, 2)),
        jnp.transpose(w_up, (1, 0, 2)),
        jnp.transpose(w_down, (2, 0, 1)),
    )
    packed, queries = lax.optimization_barrier((packed, queries))
    moved = [lax.ppermute(block, CACHE + EXPERT, along_z(piece[0])) for block, piece in zip(packed, PIECES)]

    query = queries.reshape(step_count, row_count, KVH, group_size, HD)
    query = jnp.transpose(query, (1, 0, 2, 3, 4))
    eye = jnp.eye(KVH, dtype=BF)
    query = query[:, :, :, :, None, :] * eye[None, None, :, None, :, None]
    query = query.reshape(row_count, step_count * QH, KVH * HD)
    base = (cache_place * positions).astype(jnp.int32).reshape(1)
    part = attend(lengths, base, query, k_cache, v_cache, cache_count)
    parts = lax.all_to_all(part, CACHE, split_axis=0, concat_axis=0, tiled=True)
    parts, moved[:2] = lax.optimization_barrier((parts, moved[:2]))

    own_heads = QH // cache_count
    parts = parts.reshape(cache_count, row_count, step_count, own_heads, 2 * HD)
    part_high = parts[..., HD : HD + 1]
    part_mass = parts[..., HD + 1 : HD + 2]
    factor = jnp.exp(part_high - jnp.max(part_high, axis=0))
    own_out = jnp.sum(parts[..., 0:HD] * factor, axis=0) / jnp.sum(part_mass * factor, axis=0)
    own_rows = jnp.transpose(own_out.astype(BF), (1, 0, 2, 3)).reshape(step_count * row_count, own_heads * HD)
    projected = jnp.dot(own_rows, w_out, preferred_element_type=F32).astype(BF)
    projected = jnp.broadcast_to(projected[None], (cache_count, *projected.shape))
    projected = lax.all_to_all(projected, CACHE, split_axis=0, concat_axis=0, tiled=True)
    projected, moved[2:4] = lax.optimization_barrier((projected, moved[2:4]))
    attention = jnp.sum(projected.astype(F32), axis=0)
    scale = lax.rsqrt(jnp.mean(attention * attention, axis=-1, keepdims=True) + 1e-05)
    normed = (attention * scale * norm_gain).astype(BF).reshape(step_count, row_count, D)

    experts_total = w_gate.shape[0] * cache_count
    capacity = max(2, (row_count * TOP + experts_total - 1) // experts_total)
    expert_range = jnp.arange(experts_total, dtype=jnp.int32)
    onehot = (expert_ids[..., None] == expert_range).astype(F32)
    chosen = jnp.sum(onehot, axis=2)
    gate_map = jnp.sum(onehot * gate_weights[..., None], axis=2)
    earlier = jnp.tril(jnp.ones((row_count, row_count), F32), -1)
    ranks = jnp.einsum("rq,sqe->sre", earlier, chosen, precision=lax.Precision.HIGHEST)
    slot_table = (ranks[..., None] == jnp.arange(capacity, dtype=F32)).astype(F32) * chosen[..., None]
    outgoing = jnp.einsum("srec,srd->escd", slot_table.astype(BF), normed, preferred_element_type=F32)
    outgoing = outgoing.astype(BF).reshape(experts_total, step_count * capacity, D)
    slots = lax.all_to_all(outgoing, EXPERT, split_axis=0, concat_axis=0, tiled=True)

    turns = jnp.stack([(zh - hi) % HOPS for hi, _, _ in PIECES]).astype(jnp.int32)
    joined, slots = lax.optimization_barrier((join(turns, moved), slots))
    arrived = lax.all_to_all(joined, ("core", "x", "y"), split_axis=0, concat_axis=0, tiled=True)
    partial_out = expert(slots, arrived)
    returned = lax.all_to_all(partial_out, EXPERT, split_axis=0, concat_axis=0, tiled=True)
    arrived, partial_out = lax.optimization_barrier((arrived, partial_out))
    gate_owner, up_owner, down_owner = owner(arrived)

    returned = returned.reshape(experts_total, step_count, capacity, D)
    combined = jnp.einsum(
        "srec,escd->srd",
        slot_table * gate_map[..., None],
        returned.astype(F32),
        precision=lax.Precision.HIGHEST,
    )
    shares = lax.all_gather(combined.astype(BF), CACHE, axis=0)
    total = jnp.sum(shares.astype(F32), axis=0) + attention.reshape(step_count, row_count, D)
    mixed = total.astype(BF)
    return (mixed, gate_owner.T[None], up_owner.T[None], down_owner[None])


def solution(mesh):
    return jax.shard_map(
        shards,
        mesh=Mesh(mesh.devices.reshape(4, 2, 4, 2, 4), CACHE + EXPERT),
        in_specs=(
            P(None, EXPERT, None),
            P(EXPERT, CACHE, None),
            P(EXPERT, CACHE, None),
            P(EXPERT),
            P(CACHE, None),
            P(),
            P(CACHE, EXPERT, None),
            P(CACHE, EXPERT, None),
            P(CACHE, None, EXPERT),
            P(None, EXPERT, None),
            P(None, EXPERT, None),
        ),
        out_specs=(
            P(None, EXPERT, None),
            P(EXPERT, None, CACHE),
            P(EXPERT, None, CACHE),
            P(EXPERT, CACHE, None),
        ),
        check_vma=False,
    )
```
